768 devices in a mesh: row: 32 (over z_hi, y, core), col: 24 (over z_lo, x).
Axes of the slice: x: 4, y: 8, z: 12 (z_hi: 2, z_lo: 6; z = z_hi * 6 + z_lo), core: 2. Of those that a mesh axis runs over, the one named last changes fastest.
Arguments:
- left_factors: bfloat16 [1536, 32, 512], P('col', None, 'row'), may hold values from -0.15625 to 0.15625
- right_factors: bfloat16 [1536, 4, 512], P('col'), may hold values from -0.15625 to 0.15625
- amplitudes: bfloat16 [1536, 512, 512], P('col', 'row'), may hold values from -0.46875 to 0.46875
Outputs:
- ladder: float32 [1536, 32, 4], P('col', 'row')
The draws below stay inside these ranges and needn't reach their ends.
All inputs are finite; a program needn't handle non-finite values.
Results may differ from the reference program's by a relative error of at most 0.0029.
Values may be sent and summed in bfloat16 or wider, within the bound.
No kernel may reach another device: no remote copies, remote signals or barrier semaphores. Data moves between devices by JAX's collectives and lax.ppermute only.
A program may use at most 64 MiB of HBM per device.

```python
import jax
import jax.numpy as jnp

V = 512
NAUX = 1536
NB = 4
NA = 32
NPAIR = 1536


def steps_of(own_key, dims, cuts, least, top_value):
    loudness = 1.0
    for dim, shards_of in cuts:
        heights = jax.random.uniform(jax.random.fold_in(jax.random.fold_in(own_key, 6), dim), (shards_of,), jnp.float32, least / len(cuts), top_value / len(cuts))
        loudness = loudness * jnp.repeat(jnp.exp(heights), dims[dim] // shards_of).reshape((-1,) + (1,) * (len(dims) - 1 - dim))
    return loudness


def normal_values(key, dims, width, bound, split=(), kind=jnp.bfloat16):
    drawn = width * jax.random.normal(key, dims, jnp.float32)
    if split:
        drawn = drawn * steps_of(key, dims, split, -0.22, 0.18)
    return jnp.clip(drawn, -bound, bound).astype(kind)


def setup_inputs(seed: int = 0) -> dict:
    streams_of = jax.random.split(jax.random.key(seed), 4)
    left_factors = normal_values(streams_of[0], (NAUX, NA, V), NAUX ** -0.5, 0.15625, ((0, 24), (2, 32)))
    right_factors = normal_values(streams_of[1], (NAUX, NB, V), NAUX ** -0.5, 0.15625, ((0, 24),))
    amplitudes = normal_values(streams_of[2], (NPAIR, V, V), (40.0 / V), 0.46875, ((0, 24), (1, 32)))
    return dict(left_factors=left_factors, right_factors=right_factors, amplitudes=amplitudes)


def reference(left_factors, right_factors, amplitudes):
    left_wide = left_factors.astype(jnp.float32)
    right_wide = right_factors.astype(jnp.float32)
    integrals = jnp.einsum('qac,qbd->cdab', left_wide, right_wide).astype(jnp.bfloat16)
    matrix = integrals.reshape(V * V, NA * NB)
    flat_amps = amplitudes.reshape(NPAIR, V * V)
    ladder = jnp.dot(flat_amps, matrix, preferred_element_type=jnp.float32)
    return ladder.reshape(NPAIR, NA, NB)
```

```python
import jax
import jax.numpy as jnp
from jax import lax
from jax.experimental import pallas as pl
from jax.experimental.pallas import tpu as pltpu
from jax.sharding import Mesh, PartitionSpec as P

LANES = 128
ZN, XN, CORES, ZHY = 6, 4, 2, 16


def swap(x, axis, pairs):
    return lax.ppermute(x, axis, pairs)


def exchange(x, axis):
    return lax.all_to_all(x, axis, 0, 0, tiled=True)


def in_vmem(n):
    return [pl.BlockSpec(memory_space=pltpu.VMEM)] * n


def scalar_spec():
    return pl.BlockSpec(memory_space=pltpu.SMEM)


def integrals_kernel(core_ref, mine_ref, other_ref, out_ref):
    core = core_ref[0]
    left_rows, q_half, tiles = 384, 32, 3

    def left_of(half):
        parts = []
        for x in range(XN):
            for z in range(ZN):
                start = pl.multiple_of(z * 64 + half * q_half, q_half)
                parts.append(mine_ref[x, pl.ds(start, q_half), :])
        return jnp.concatenate(parts, axis=0)

    def right_of(ref, base):
        cols = []
        for s in range(tiles):
            rows = [ref[x, pl.ds(base + s * 192, 192), :] for x in range(XN)]
            cols.append(jnp.concatenate(rows, axis=0))
        return jnp.concatenate(cols, axis=1)

    dims = (((0,), (0,)), ((), ()))
    acc = lax.dot_general(left_of(core), right_of(mine_ref, left_rows), dims, preferred_element_type=jnp.float32)
    acc = acc + lax.dot_general(left_of(1 - core), right_of(other_ref, 0), dims, preferred_element_type=jnp.float32)
    tile = acc.astype(jnp.bfloat16)
    for z in range(ZN):
        out_ref[z] = tile


def ladder_kernel(x_ref, ints_ref, t0_ref, t1_ref, t2_ref, t3_ref, out_ref):
    x = x_ref[0]
    t_refs = (t0_ref, t1_ref, t2_ref, t3_ref)
    acc = jnp.zeros((LANES, 256), jnp.float32)
    for c in range(4):
        rows = []
        for b in range(4):
            cols = []
            for dt in range(4):
                j = 4 * b + dt
                cols.append(ints_ref[j // 3, c * 32 : c * 32 + 32, (j % 3) * LANES : (j % 3 + 1) * LANES])
            rows.append(jnp.concatenate(cols, axis=1))
        rhs = jnp.concatenate(rows, axis=0)
        amps = jnp.concatenate([t[c] for t in t_refs], axis=0)
        acc = acc + lax.dot_general(rhs, amps, (((1,), (1,)), ((), ())), preferred_element_type=jnp.float32)
    for s in range(4):
        to = lax.rem(x + 4 - s, 4)
        for b in range(4):
            for core in range(CORES):
                r = b * 32 + core * 16
                out_ref[core, to, :, b, :] = acc[r : r + 16, s * 64 : s * 64 + 64]


def per_device(left, right, amps):
    core = lax.axis_index("core")
    x = lax.axis_index("x")
    def chunk(s):
        to = lax.rem(x + s, 4)
        part = lax.dynamic_slice_in_dim(amps, to * 4, 4, axis=1)
        return jnp.transpose(part, (1, 0, 2))

    t_parts = [chunk(0)]
    for s in range(1, 4):
        t_parts.append(lax.ppermute(chunk(s), "x", [(i, (i + s) % 4) for i in range(4)]))
    q = left.shape[0]
    lt = jnp.transpose(left.reshape(q, ZHY, CORES, XN, 4), (3, 0, 4, 2, 1)).reshape(1, XN * q, LANES)
    rh = lax.dynamic_slice_in_dim(right, core * 32, 32, axis=0).reshape(32, 16, LANES)
    rh = jnp.pad(jnp.transpose(rh, (1, 0, 2)), ((0, 2), (0, 0), (0, 0))).reshape(ZN, 96, LANES)
    z1 = exchange(jnp.concatenate([jnp.broadcast_to(lt, (ZN, XN * q, LANES)), rh], axis=1), "zl")
    lz = jnp.transpose(z1[:, : XN * q].reshape(ZN, XN, q, LANES), (1, 0, 2, 3)).reshape(XN, ZN * q, LANES)
    rz = jnp.transpose(z1[:, XN * q :].reshape(ZN, 3, 32, LANES), (1, 0, 2, 3)).reshape(1, 576, LANES)
    x1 = exchange(jnp.concatenate([lz, jnp.broadcast_to(rz, (XN, 576, LANES))], axis=1), "x")
    other = lax.ppermute(x1[:, 384:], "core", [(0, 1), (1, 0)])
    ints = pl.pallas_call(
        integrals_kernel,
        out_shape=jax.ShapeDtypeStruct((ZN, LANES, 384), jnp.bfloat16),
        in_specs=[scalar_spec(), *in_vmem(2)],
        out_specs=in_vmem(1)[0],
        name="integrals",
    )(core.reshape(1), x1, other)
    ints = exchange(ints, "zl")
    part = pl.pallas_call(
        ladder_kernel,
        out_shape=jax.ShapeDtypeStruct((CORES, XN, ZHY, 4, 64), jnp.float32),
        in_specs=[scalar_spec(), *in_vmem(5)],
        out_specs=in_vmem(1)[0],
        name="ladder",
    )(x.reshape(1), ints, *t_parts)
    part = exchange(part.reshape(CORES * XN, ZHY, 4, 64), ("core", "x")).sum(axis=0)
    part = exchange(part, ("zh", "y")).sum(axis=0)
    return jnp.transpose(part, (1, 0))[:, None, :]


def solution(mesh):
    fine = Mesh(mesh.devices.reshape(2, 8, CORES, ZN, XN), ("zh", "y", "core", "zl", "x"))
    row, col = ("zh", "y", "core"), ("zl", "x")
    placed = (P(col, None, row), P(col, None, None), P(col, row, None))
    return jax.shard_map(per_device, mesh=fine, in_specs=placed, out_specs=P(col, row, None), check_vma=False)
```

```python
import jax
import jax.numpy as jnp
from jax import lax
from jax.experimental import pallas as pl
from jax.experimental.pallas import tpu as pltpu
from jax.sharding import Mesh, PartitionSpec as P


LANES = 128
ZH, YN, CORES, ZN, XN = 2, 8, 2, 6, 4
ZHY = ZH * YN
XC, XD = 2, 2
HALF = 32
C_PART, D_PART = 8, 256
SLOTS = 4
KERNEL_VMEM = 60 * 1024 * 1024


def exchange(x, axis):
    return lax.all_to_all(x, axis, 0, 0, tiled=True)


def ladder_kernel(where_ref, *refs):
    hbm, out_ref, (left_ref, right_ref, amps_ref, sems) = refs[:13], refs[13], refs[14:]
    core, y, x = where_ref[0], where_ref[1], where_ref[2]
    targets = [left_ref] + [right_ref.at[i] for i in range(2 * SLOTS)] + [amps_ref.at[s] for s in range(XN)]
    copies = [pltpu.make_async_copy(a, b, sems.at[i]) for i, (a, b) in enumerate(zip(hbm, targets))]
    for copy in copies:
        copy.start()

    def left_of(half):
        start = pl.multiple_of(half * HALF, HALF)
        parts = [left_ref[i, z, pl.ds(start, HALF), :] for z in range(ZN) for i in range(XN)]
        return jnp.concatenate(parts, axis=0)

    def right_of(who):
        cols = []
        for slot in range(SLOTS):
            for t in range(2):
                rows = [right_ref[who * SLOTS + slot, k, t] for k in range(ZN * XN)]
                cols.append(jnp.concatenate(rows, axis=0))
        return jnp.concatenate(cols, axis=1)

    dims = (((0,), (0,)), ((), ()))
    for copy in copies[: 1 + SLOTS]:
        copy.wait()
    ints = lax.dot_general(left_of(core), right_of(0), dims, preferred_element_type=jnp.float32)
    for copy in copies[1 + SLOTS : 1 + 2 * SLOTS]:
        copy.wait()
    ints = ints + lax.dot_general(left_of(1 - core), right_of(1), dims, preferred_element_type=jnp.float32)
    ints = ints.astype(jnp.bfloat16)
    for copy in copies[1 + 2 * SLOTS :]:
        copy.wait()
    acc = jnp.zeros((LANES, 256), jnp.float32)
    for c in range(C_PART):
        rhs = jnp.concatenate(
            [ints[c * 32 : c * 32 + 32, i * D_PART : (i + 1) * D_PART] for i in range(SLOTS)], axis=0
        )
        amps = jnp.concatenate([amps_ref[s, c] for s in range(XN)], axis=0)
        acc = acc + lax.dot_general(rhs, amps, (((1,), (1,)), ((), ())), preferred_element_type=jnp.float32)
    for slot in range(SLOTS):
        row = pl.multiple_of(lax.rem(y + slot, SLOTS) * YN, YN)
        for s in range(XN):
            to = lax.rem(x + XN - s, XN)
            for k in range(CORES):
                r = slot * 32 + k * 16
                both = [acc[r + h * YN : r + h * YN + YN, s * 64 : s * 64 + 64] for h in range(ZH)]
                out_ref[k * XN + to, pl.ds(row, YN), :] = jnp.concatenate(both, axis=1)


def fold_kernel(in_ref, out_ref):
    total = in_ref[0]
    for i in range(1, CORES * XN):
        total = total + in_ref[i]
    turned = jnp.concatenate([total[:, 64:], total[:, :64]], axis=1)
    for b in range(4):
        for h, rows in enumerate((total, turned)):
            out_ref[h * YN : h * YN + YN, b, :] = rows[b * YN : b * YN + YN, :]


def ladder_part(left, right, amps):
    core = lax.axis_index("core")
    x = lax.axis_index("x")
    y = lax.axis_index("y")
    q, width = left.shape[0], right.shape[2]
    pairs = [(0, 1), (1, 0)]

    def quarter(s):
        to = lax.rem(x + s, XN)
        start = (0, (to // XD) * C_PART, lax.rem(to, XD) * D_PART)
        return jnp.transpose(lax.dynamic_slice(amps, start, (64, C_PART, D_PART)), (1, 0, 2))

    t_parts = [quarter(0)]
    for s in range(1, XN):
        t_parts.append(lax.ppermute(quarter(s), "x", [(i, (i + s) % XN) for i in range(XN)]))
    part = lax.dynamic_slice(right, (core * HALF, lax.rem(y, SLOTS), 0), (HALF, 1, width))
    part = jnp.transpose(part.reshape(HALF, XD, 2, LANES), (1, 2, 0, 3))
    part = jnp.broadcast_to(part[None, None], (ZN, XC, *part.shape)).reshape(ZN * XN, 2, HALF, LANES)
    r0 = exchange(part, ("zl", "x"))
    lt = jnp.transpose(left.reshape(q, ZHY, CORES, 16), (0, 3, 2, 1)).reshape(q, XC, 256)
    lt = jnp.broadcast_to(jnp.transpose(lt, (1, 0, 2))[None], (ZN, XC, q, 256))
    lt, r0 = lax.optimization_barrier((lt, r0))
    lz = exchange(lt, "zl")
    hops = (
        [(i, (i - 1) % YN) for i in range(YN)],
        [(i, (i + (2 if i % 2 == 0 else -2)) % YN) for i in range(YN)],
        [(i, (i + 1) % YN) for i in range(YN)],
    )
    mine = [r0] + [lax.ppermute(r0, "y", hop) for hop in hops]
    lx = jnp.broadcast_to(jnp.transpose(lz, (1, 0, 2, 3))[:, None], (XC, XD, ZN, q, 256)).reshape(XN, ZN, q, 256)
    first = lax.ppermute(r0, "core", pairs)
    lx, first, t_parts = lax.optimization_barrier((lx, first, t_parts))
    lx = exchange(lx, "x")
    other = [first] + [lax.ppermute(r, "core", pairs) for r in mine[1:]]
    vmem = pl.BlockSpec(memory_space=pltpu.VMEM)
    hbm = pl.BlockSpec(memory_space=pl.ANY)
    part = pl.pallas_call(
        ladder_kernel,
        out_shape=jax.ShapeDtypeStruct((CORES * XN, 32, LANES), jnp.float32),
        in_specs=[pl.BlockSpec(memory_space=pltpu.SMEM)] + [hbm] * 13,
        out_specs=vmem,
        scratch_shapes=[
            pltpu.VMEM(lx.shape, lx.dtype),
            pltpu.VMEM((2 * SLOTS, *r0.shape), r0.dtype),
            pltpu.VMEM((XN, C_PART, 64, D_PART), amps.dtype),
            pltpu.SemaphoreType.DMA((13,)),
        ],
        compiler_params=pltpu.CompilerParams(vmem_limit_bytes=KERNEL_VMEM),
        name="ladder",
    )(jnp.stack([core, y, x]), lx, *mine, *other, *t_parts)
    part = exchange(part, ("core", "x"))
    part = pl.pallas_call(
        fold_kernel,
        out_shape=jax.ShapeDtypeStruct((ZHY, 4, LANES), jnp.float32),
        in_specs=[vmem],
        out_specs=vmem,
        compiler_params=pltpu.CompilerParams(vmem_limit_bytes=4 * 1024 * 1024),
        name="fold",
    )(part)
    part = exchange(part, ("zh", "y")).sum(axis=0)[:, :64]
    return jnp.transpose(part, (1, 0))[:, None, :]


def solution(mesh):
    fine = Mesh(mesh.devices.reshape(ZH, YN, CORES, ZN, XN), ("zh", "y", "core", "zl", "x"))
    row, col = ("zh", "y", "core"), ("zl", "x")
    placed = (P(col, None, row), P(col, None, None), P(col, row, None))
    return jax.shard_map(ladder_part, mesh=fine, in_specs=placed, out_specs=P(col, row, None), check_vma=False)
```

```python
import jax
import jax.numpy as jnp
from jax import lax
from jax.experimental import pallas as pl
from jax.experimental.pallas import tpu as pltpu
from jax.sharding import Mesh, PartitionSpec as P


LANES = 128
ZH, YN, CORES, ZN, XN = 2, 8, 2, 6, 4
ZHY = ZH * YN
HALF = 32
SLOTS = 4
L_ROWS = 256
KERNEL_VMEM = 50 * 1024 * 1024


def exchange(x, axis):
    return lax.all_to_all(x, axis, 0, 0, tiled=True)


def ladder_kernel(where_ref, left_ref, r0_ref, r1_ref, o0_ref, o1_ref, *refs):
    amps_hbm, out_ref, (amps_ref, sems) = refs[:XN], refs[XN], refs[XN + 1 :]
    core, y, x = where_ref[0], where_ref[1], where_ref[2]
    copies = [pltpu.make_async_copy(t, amps_ref.at[s], sems.at[s]) for s, t in enumerate(amps_hbm)]
    for copy in copies:
        copy.start()

    def left_of(half):
        cols = []
        for j in range(4):
            start = pl.multiple_of(j * 64 + half * HALF, HALF)
            rows = [left_ref[i, z, pl.ds(start, HALF), :] for z in range(ZN) for i in range(XN)]
            cols.append(jnp.concatenate(rows, axis=0))
        return jnp.concatenate(cols, axis=1)

    def right_of(own, rest):
        return jnp.concatenate([own[...]] + [rest[i] for i in range(SLOTS - 1)], axis=1)

    dims = (((0,), (0,)), ((), ()))
    ints = lax.dot_general(left_of(core), right_of(r0_ref, r1_ref), dims, preferred_element_type=jnp.float32)
    ints = ints + lax.dot_general(left_of(1 - core), right_of(o0_ref, o1_ref), dims, preferred_element_type=jnp.float32)
    ints = ints.astype(jnp.bfloat16)
    for copy in copies:
        copy.wait()
    acc = jnp.zeros((LANES, 256), jnp.float32)
    for c in range(0, 16, 2):
        pair = []
        for k in (c, c + 1):
            cols = [ints[k * 32 : k * 32 + 32, i * LANES : (i + 1) * LANES] for i in range(SLOTS)]
            pair.append(jnp.concatenate(cols, axis=0))
        amps = [jnp.concatenate([amps_ref[s, k] for s in range(XN)], axis=0) for k in (c, c + 1)]
        acc = acc + lax.dot_general(
            jnp.concatenate(pair, axis=1),
            jnp.concatenate(amps, axis=1),
            (((1,), (1,)), ((), ())),
            preferred_element_type=jnp.float32,
        )
    for slot in range(SLOTS):
        row = pl.multiple_of(lax.rem(y + slot, SLOTS) * YN, YN)
        for s in range(XN):
            to = lax.rem(x + XN - s, XN)
            for k in range(CORES):
                r = slot * 32 + k * 16
                both = [acc[r + h * YN : r + h * YN + YN, s * 64 : s * 64 + 64] for h in range(ZH)]
                out_ref[k * XN + to, pl.ds(row, YN), :] = jnp.concatenate(both, axis=1)


def fold_kernel(in_ref, out_ref):
    total = in_ref[0]
    for i in range(1, CORES * XN):
        total = total + in_ref[i]
    turned = jnp.concatenate([total[:, 64:], total[:, :64]], axis=1)
    for b in range(4):
        for h, rows in enumerate((total, turned)):
            out_ref[h * YN : h * YN + YN, b, :] = rows[b * YN : b * YN + YN, :]


def ladder_part(left, right, amps):
    core = lax.axis_index("core")
    x = lax.axis_index("x")
    y = lax.axis_index("y")
    q, width = left.shape[0], right.shape[2]
    pairs = [(0, 1), (1, 0)]

    part = lax.dynamic_slice(right, (core * HALF, lax.rem(y, SLOTS), 0), (HALF, 1, width))
    part = jnp.transpose(part.reshape(HALF, XN, LANES), (1, 0, 2))
    rx = exchange(part, "x").reshape(1, XN * HALF, LANES)

    def quarter(s):
        start = lax.rem(x + s, XN) * LANES
        return jnp.transpose(lax.dynamic_slice_in_dim(amps, start, LANES, axis=2), (1, 0, 2))

    t_parts = [quarter(0)]
    for s in range(1, XN):
        t_parts.append(lax.ppermute(quarter(s), "x", [(i, (i + s) % XN) for i in range(XN)]))
    lt = jnp.transpose(left.reshape(q, ZHY, CORES, 16), (0, 3, 2, 1)).reshape(q, 4, LANES)
    lt = jnp.transpose(lt, (1, 0, 2)).reshape(1, L_ROWS, LANES)
    both = jnp.concatenate([lt, rx], axis=1)
    both = exchange(jnp.broadcast_to(both, (ZN, *both.shape[1:])), "zl")
    r0 = both[:, L_ROWS:].reshape(ZN * XN * HALF, LANES)
    lx = jnp.broadcast_to(both[None, :, :L_ROWS], (XN, ZN, L_ROWS, LANES))
    lx, r0, t_parts = lax.optimization_barrier((lx, r0, t_parts))
    lx = exchange(lx, "x")
    hops = (
        [(i, (i - 1) % YN) for i in range(YN)],
        [(i, (i + (2 if i % 2 == 0 else -2)) % YN) for i in range(YN)],
        [(i, (i + 1) % YN) for i in range(YN)],
    )
    r1 = [lax.ppermute(r0, "y", hop) for hop in hops]
    o0 = lax.ppermute(r0, "core", pairs)
    r1 = jnp.stack(r1)
    o1 = lax.ppermute(r1, "core", pairs)
    vmem = pl.BlockSpec(memory_space=pltpu.VMEM)
    hbm = pl.BlockSpec(memory_space=pl.ANY)
    part = pl.pallas_call(
        ladder_kernel,
        out_shape=jax.ShapeDtypeStruct((CORES * XN, 32, LANES), jnp.float32),
        in_specs=[pl.BlockSpec(memory_space=pltpu.SMEM)] + [vmem] * 5 + [hbm] * XN,
        out_specs=vmem,
        scratch_shapes=[
            pltpu.VMEM((XN, 16, 64, LANES), amps.dtype),
            pltpu.SemaphoreType.DMA((XN,)),
        ],
        compiler_params=pltpu.CompilerParams(vmem_limit_bytes=KERNEL_VMEM),
        name="ladder",
    )(jnp.stack([core, y, x]), lx, r0, r1, o0, o1, *t_parts)
    part = exchange(part, ("core", "x"))
    part = pl.pallas_call(
        fold_kernel,
        out_shape=jax.ShapeDtypeStruct((ZHY, 4, LANES), jnp.float32),
        in_specs=[vmem],
        out_specs=vmem,
        compiler_params=pltpu.CompilerParams(vmem_limit_bytes=4 * 1024 * 1024),
        name="fold",
    )(part)
    part = exchange(part, ("zh", "y")).sum(axis=0)[:, :64]
    return jnp.transpose(part, (1, 0))[:, None, :]


def solution(mesh):
    fine = Mesh(mesh.devices.reshape(ZH, YN, CORES, ZN, XN), ("zh", "y", "core", "zl", "x"))
    row, col = ("zh", "y", "core"), ("zl", "x")
    placed = (P(col, None, row), P(col, None, None), P(col, row, None))
    return jax.shard_map(ladder_part, mesh=fine, in_specs=placed, out_specs=P(col, row, None), check_vma=False)
```

```python
import jax
import jax.numpy as jnp
from jax import lax
from jax.experimental import pallas as pl
from jax.experimental.pallas import tpu as pltpu
from jax.sharding import Mesh, PartitionSpec as P


LANES = 128
ZH, YN, CORES, ZN, XN = 2, 8, 2, 6, 4
ZHY = ZH * YN
HALF = 32
SLOTS = 4
L_ROWS = 256
KERNEL_VMEM = 50 * 1024 * 1024


def exchange(x, axis):
    return lax.all_to_all(x, axis, 0, 0, tiled=True)


def ladder_kernel(where_ref, left_ref, r0_ref, r1_ref, o0_ref, o1_ref, *refs):
    amps_hbm, out_ref, (amps_ref, sems) = refs[:XN], refs[XN], refs[XN + 1 :]
    core, y, x = where_ref[0], where_ref[1], where_ref[2]
    copies = [pltpu.make_async_copy(t, amps_ref.at[s], sems.at[s]) for s, t in enumerate(amps_hbm)]
    for copy in copies:
        copy.start()

    def left_of(half):
        cols = []
        for j in range(4):
            start = pl.multiple_of(j * 64 + half * HALF, HALF)
            rows = [left_ref[i, z, pl.ds(start, HALF), :] for z in range(ZN) for i in range(XN)]
            cols.append(jnp.concatenate(rows, axis=0))
        return jnp.concatenate(cols, axis=1)

    def right_of(own, rest):
        return jnp.concatenate([own[...]] + [rest[i] for i in range(SLOTS - 1)], axis=1)

    dims = (((0,), (0,)), ((), ()))
    ints = lax.dot_general(left_of(core), right_of(r0_ref, r1_ref), dims, preferred_element_type=jnp.float32)
    ints = ints + lax.dot_general(left_of(1 - core), right_of(o0_ref, o1_ref), dims, preferred_element_type=jnp.float32)
    ints = ints.astype(jnp.bfloat16)
    for copy in copies:
        copy.wait()
    acc = jnp.zeros((LANES, 256), jnp.float32)
    for c in range(0, 16, 2):
        pair = []
        for k in (c, c + 1):
            cols = [ints[k * 32 : k * 32 + 32, i * LANES : (i + 1) * LANES] for i in range(SLOTS)]
            pair.append(jnp.concatenate(cols, axis=0))
        amps = [jnp.concatenate([amps_ref[s, k] for s in range(XN)], axis=0) for k in (c, c + 1)]
        acc = acc + lax.dot_general(
            jnp.concatenate(pair, axis=1),
            jnp.concatenate(amps, axis=1),
            (((1,), (1,)), ((), ())),
            preferred_element_type=jnp.float32,
        )
    for slot in range(SLOTS):
        row = pl.multiple_of(lax.rem(y + slot, SLOTS) * YN, YN)
        for s in range(XN):
            to = lax.rem(x + XN - s, XN)
            for k in range(CORES):
                r = slot * 32 + k * 16
                both = [acc[r + h * YN : r + h * YN + YN, s * 64 : s * 64 + 64] for h in range(ZH)]
                out_ref[k * XN + to, pl.ds(row, YN), :] = jnp.concatenate(both, axis=1)


def pack_kernel(left_ref, right_ref, out_ref, sems):
    rows = (pl.ds(0, L_ROWS), pl.ds(L_ROWS, XN * HALF))
    copies = []
    for z in range(ZN):
        for i, ref in enumerate((left_ref, right_ref)):
            copies.append(pltpu.make_async_copy(ref, out_ref.at[z, rows[i], :], sems.at[2 * z + i]))
    for copy in copies:
        copy.start()
    for copy in copies:
        copy.wait()


def spread_kernel(in_ref, left_ref, right_ref, sems):
    copies = [pltpu.make_async_copy(in_ref.at[:, pl.ds(L_ROWS, XN * HALF), :], right_ref, sems.at[XN])]
    for i in range(XN):
        copies.append(pltpu.make_async_copy(in_ref.at[:, pl.ds(0, L_ROWS), :], left_ref.at[i], sems.at[i]))
    for copy in copies:
        copy.start()
    for copy in copies:
        copy.wait()


def fold_kernel(in_ref, out_ref):
    total = in_ref[0]
    for i in range(1, CORES * XN):
        total = total + in_ref[i]
    turned = jnp.concatenate([total[:, 64:], total[:, :64]], axis=1)
    for b in range(4):
        for h, rows in enumerate((total, turned)):
            out_ref[h * YN : h * YN + YN, b, :] = rows[b * YN : b * YN + YN, :]


def ladder_part(left, right, amps):
    core = lax.axis_index("core")
    x = lax.axis_index("x")
    y = lax.axis_index("y")
    q, width = left.shape[0], right.shape[2]
    pairs = [(0, 1), (1, 0)]

    part = lax.dynamic_slice(right, (core * HALF, lax.rem(y, SLOTS), 0), (HALF, 1, width))
    part = jnp.transpose(part.reshape(HALF, XN, LANES), (1, 0, 2))
    rx = exchange(part, "x").reshape(XN * HALF, LANES)

    def quarter(s):
        start = lax.rem(x + s, XN) * LANES
        return jnp.transpose(lax.dynamic_slice_in_dim(amps, start, LANES, axis=2), (1, 0, 2))

    t_parts = [quarter(0)]
    for s in range(1, XN):
        t_parts.append(lax.ppermute(quarter(s), "x", [(i, (i + s) % XN) for i in range(XN)]))
    lt = jnp.transpose(left.reshape(q, ZHY, CORES, 16), (0, 3, 2, 1)).reshape(q, 4, LANES)
    lt = jnp.transpose(lt, (1, 0, 2)).reshape(L_ROWS, LANES)
    anywhere = pl.BlockSpec(memory_space=pl.ANY)
    small = pltpu.CompilerParams(vmem_limit_bytes=1024 * 1024)
    both = pl.pallas_call(
        pack_kernel,
        out_shape=jax.ShapeDtypeStruct((ZN, L_ROWS + XN * HALF, LANES), left.dtype),
        in_specs=[anywhere] * 2,
        out_specs=anywhere,
        scratch_shapes=[pltpu.SemaphoreType.DMA((2 * ZN,))],
        compiler_params=small,
        name="pack",
    )(lt, rx)
    both = exchange(both, "zl")
    lx, r0 = pl.pallas_call(
        spread_kernel,
        out_shape=(
            jax.ShapeDtypeStruct((XN, ZN, L_ROWS, LANES), left.dtype),
            jax.ShapeDtypeStruct((ZN, XN * HALF, LANES), left.dtype),
        ),
        in_specs=[anywhere],
        out_specs=(anywhere, anywhere),
        scratch_shapes=[pltpu.SemaphoreType.DMA((XN + 1,))],
        compiler_params=small,
        name="spread",
    )(both)
    r0 = r0.reshape(ZN * XN * HALF, LANES)
    lx, r0 = lax.optimization_barrier((lx, r0))
    lx = exchange(lx, "x")
    hops = (
        [(i, (i - 1) % YN) for i in range(YN)],
        [(i, (i + (2 if i % 2 == 0 else -2)) % YN) for i in range(YN)],
        [(i, (i + 1) % YN) for i in range(YN)],
    )
    r1 = []
    for hop in hops:
        r1.append(lax.ppermute(r0, "y", hop))
    o0 = lax.ppermute(r0, "core", pairs)
    r1 = jnp.stack(r1)
    o1 = lax.ppermute(r1, "core", pairs)
    vmem = pl.BlockSpec(memory_space=pltpu.VMEM)
    hbm = pl.BlockSpec(memory_space=pl.ANY)
    part = pl.pallas_call(
        ladder_kernel,
        out_shape=jax.ShapeDtypeStruct((CORES * XN, 32, LANES), jnp.float32),
        in_specs=[pl.BlockSpec(memory_space=pltpu.SMEM)] + [vmem] * 5 + [hbm] * XN,
        out_specs=vmem,
        scratch_shapes=[
            pltpu.VMEM((XN, 16, 64, LANES), amps.dtype),
            pltpu.SemaphoreType.DMA((XN,)),
        ],
        compiler_params=pltpu.CompilerParams(vmem_limit_bytes=KERNEL_VMEM),
        name="ladder",
    )(jnp.stack([core, y, x]), lx, r0, r1, o0, o1, *t_parts)
    part = exchange(part, ("core", "x"))
    part = pl.pallas_call(
        fold_kernel,
        out_shape=jax.ShapeDtypeStruct((ZHY, 4, LANES), jnp.float32),
        in_specs=[vmem],
        out_specs=vmem,
        compiler_params=pltpu.CompilerParams(vmem_limit_bytes=4 * 1024 * 1024),
        name="fold",
    )(part)
    part = exchange(part, ("zh", "y")).sum(axis=0)[:, :64]
    return jnp.transpose(part, (1, 0))[:, None, :]


def solution(mesh):
    fine = Mesh(mesh.devices.reshape(ZH, YN, CORES, ZN, XN), ("zh", "y", "core", "zl", "x"))
    row, col = ("zh", "y", "core"), ("zl", "x")
    placed = (P(col, None, row), P(col, None, None), P(col, row, None))
    return jax.shard_map(ladder_part, mesh=fine, in_specs=placed, out_specs=P(col, row, None), check_vma=False)
```
